32 devices in a mesh: box: 4 (over y, x), dir: 8 (over z, core).
Axes of the slice: x: 2, y: 2, z: 4, core: 2. Of those that a mesh axis runs over, the one named last changes fastest.
Arguments:
- currents: bfloat16 [2048, 512], P(('box', 'dir')), may hold values from -6 to 6
- near_list: int32 [2048, 27], P(('box', 'dir')), may hold values from 0 to 2047, as said below
- far_list: int32 [256, 20], replicated, may hold values from 0 to 255, as said below
- far_kind: int32 [256, 20], replicated, may hold values from 0 to 315
- aggregate: bfloat16 [512, 1024], replicated, may hold values from -0.25 to 0.25
- interp: bfloat16 [1024, 4096], replicated, may hold values from -0.1875 to 0.1875
- receive: bfloat16 [1024, 512], replicated, may hold values from -0.1875 to 0.1875
- shift_angle: float32 [8, 2048], replicated, may hold values from -3.140625 to 3.140625
- translation: float32 [316, 2, 2048], P(None, None, 'dir'), may hold values from -0.6 to 0.6
- near_matrix: bfloat16 [27, 512, 512], replicated, may hold values from -0.0546875 to 0.0546875
Outputs:
- fields: float32 [2048, 512], P(('box', 'dir'))
The draws below stay inside these ranges and needn't reach their ends.
Inputs may be any that keep to these rules, and one draw needn't show every extreme that they name: `near_list`: entry [l, n] lies within 32 of l. `far_list`: entry [p, j] differs from p by 2 to 32.
All inputs are finite; a program needn't handle non-finite values.
Results may differ from the reference program's by a relative error of at most 0.013.
Values may be sent and summed in bfloat16 or wider, within the bound.
A program may use at most 128 MiB of HBM per device.

```python
import jax
import jax.numpy as jnp
from jax import lax

CUR = 256
Q0 = 512
Q1 = 2048
KINDS = 316
FAR = 20
NEAR = 27
LEAVES = 2048
PARENTS = 256
REACH = 32
FAR_REACH = 32


def draw_near_list(key, part):
    leaf_index = jnp.arange(LEAVES, dtype=jnp.int32)[:, None]
    offset = jax.random.randint(jax.random.fold_in(key, 7), (LEAVES, NEAR), -REACH, REACH + 1, dtype=jnp.int32)
    return jnp.clip(leaf_index + offset, 0, LEAVES - 1).astype(jnp.int32)


def far_pairs(key):
    base = jax.random.fold_in(key, 31)
    magnitude = jax.random.randint(jax.random.fold_in(base, 1), (PARENTS, FAR), 2, FAR_REACH + 1, dtype=jnp.int32)
    sign_draw = jax.random.randint(jax.random.fold_in(base, 2), (PARENTS, FAR), 0, 2, dtype=jnp.int32)
    offset = magnitude * (2 * sign_draw - 1)
    parent_index = jnp.arange(PARENTS, dtype=jnp.int32)[:, None]
    target = parent_index + offset
    offset = jnp.where((target < 0) | (target >= PARENTS), -offset, offset)
    return (parent_index + offset).astype(jnp.int32)


def draw_far_list(key, part):
    targets = far_pairs(key)
    return targets


def draw_far_kind(key, part):
    kinds = jax.random.randint(jax.random.fold_in(key, 53), (PARENTS, FAR), 0, KINDS, dtype=jnp.int32)
    kinds = kinds.at[0, 0].set(KINDS - 1)
    kinds = kinds.at[0, 1].set(0)
    return kinds.astype(jnp.int32)


def levels(rng, dims, cuts, low, top_value):
    def one(dim, blocks):
        draws = jax.random.uniform(jax.random.fold_in(jax.random.fold_in(rng, 6), dim), (blocks,), jnp.float32, low / len(cuts), top_value / len(cuts))
        return jnp.repeat(jnp.exp(draws), dims[dim] // blocks).reshape((-1,) + (1,) * (len(dims) - dim - 1))

    loudness = one(*cuts[0])
    for cut in cuts[1:]:
        loudness = loudness * one(*cut)
    return loudness


def noise(rng, extent, width, limit, cuts=(), kind=jnp.bfloat16):
    values = jax.random.normal(rng, extent, jnp.float32) * width
    if len(cuts) > 0:
        values = levels(rng, extent, cuts, -0.22, 0.18) * values
    return jnp.clip(values, min=-limit, max=limit).astype(kind)


def setup_inputs(seed: int = 0) -> dict:
    arg_keys = jax.random.split(jax.random.key(seed), 11)
    currents = noise(arg_keys[0], (LEAVES, 2 * CUR), 1.0, 6.0, ((0, 32),))
    near_list = draw_near_list(jax.random.fold_in(arg_keys[10], 71), 0)
    far_list = draw_far_list(jax.random.fold_in(arg_keys[10], 71), 0)
    far_kind = draw_far_kind(jax.random.fold_in(arg_keys[10], 71), 0)
    aggregate = noise(arg_keys[4], (2 * CUR, 2 * Q0), (2 * CUR) ** -0.5, 0.25)
    interp = noise(arg_keys[5], (2 * Q0, 2 * Q1), (2 * Q0) ** -0.5, 0.1875)
    receive = noise(arg_keys[6], (2 * Q0, 2 * CUR), (2 * Q0) ** -0.5, 0.1875)
    shift_angle = jnp.clip(jax.random.uniform(arg_keys[7], (8, Q1), jnp.float32, -3.140625, 3.140625), -3.140625, 3.140625)
    translation = noise(arg_keys[8], (KINDS, 2, Q1), 0.1, 0.6, ((2, 8),), jnp.float32)
    near_matrix = noise(arg_keys[9], (NEAR, 2 * CUR, 2 * CUR), (2 * CUR * NEAR) ** -0.5, 0.0546875)
    return {"currents": currents, "near_list": near_list, "far_list": far_list, "far_kind": far_kind, "aggregate": aggregate, "interp": interp, "receive": receive, "shift_angle": shift_angle, "translation": translation, "near_matrix": near_matrix}


def reference(currents, near_list, far_list, far_kind, aggregate, interp, receive, shift_angle, translation, near_matrix):
    leaves = currents.shape[0]
    parents = leaves // 8
    pattern = jnp.dot(currents, aggregate, preferred_element_type=jnp.float32).astype(jnp.bfloat16)
    children = jnp.dot(pattern, interp, preferred_element_type=jnp.float32).reshape(parents, 8, 2, Q1)
    cosine = jnp.cos(shift_angle)
    sine_part = jnp.sin(shift_angle)
    real_part = jnp.sum(children[:, :, 0] * cosine - children[:, :, 1] * sine_part, axis=1)
    imag_part = jnp.sum(children[:, :, 0] * sine_part + children[:, :, 1] * cosine, axis=1)
    local_real = jnp.zeros((parents, Q1), jnp.float32)
    local_imag = jnp.zeros((parents, Q1), jnp.float32)
    for slot in range(FAR):
        source_real = real_part[far_list[:, slot]]
        source_imag = imag_part[far_list[:, slot]]
        operator = translation[far_kind[:, slot]]
        local_real = local_real + operator[:, 0] * source_real - operator[:, 1] * source_imag
        local_imag = local_imag + operator[:, 0] * source_imag + operator[:, 1] * source_real
    rot_real = local_real[:, None] * cosine + local_imag[:, None] * sine_part
    rot_imag = local_imag[:, None] * cosine - local_real[:, None] * sine_part
    received = jnp.stack([rot_real, rot_imag], axis=2).reshape(leaves, 2 * Q1).astype(jnp.bfloat16)
    back_pattern = lax.dot_general(received, interp, (((1,), (1,)), ((), ())), preferred_element_type=jnp.float32).astype(jnp.bfloat16)
    fields = jnp.dot(back_pattern, receive, preferred_element_type=jnp.float32)
    for slot in range(NEAR):
        fields = fields + jnp.dot(currents[near_list[:, slot]], near_matrix[slot], preferred_element_type=jnp.float32)
    return fields
```

```python
import functools

import jax
import jax.numpy as jnp
from jax import lax
from jax.experimental import pallas as pl
from jax.experimental.pallas import tpu as pltpu
from jax.sharding import PartitionSpec as P

MESH = pl.DeviceIdType.MESH
LANES = 128
F32 = jnp.float32
BF16 = jnp.bfloat16


def kernel(
    boxes,
    dirs,
    far_ref,
    kind_ref,
    currents,
    near_list,
    shift_angle,
    aggregate,
    interp,
    receive,
    translation,
    near_matrix,
    out,
    agg_vm,
    interp_vm,
    receive_vm,
    trans_vm,
    near_vm,
    padded,
    near_index,
    cosine,
    sine_part,
    pattern,
    send_up,
    upper,
    operator,
    source,
    local,
    send_back,
    returned,
    near_acc,
    back_acc,
    misc_sem,
    interp_sem,
    near_sem,
    halo_send,
    halo_recv,
    up_send,
    up_recv,
    back_send,
    back_recv,
):
    box = lax.axis_index("box")
    me = lax.axis_index("dir")
    leaf_dev, cur = currents.shape
    own = leaf_dev // 8
    reach = leaf_dev // 2
    half = dirs // 2
    slots, _, _ = near_matrix.shape
    directions = shift_angle.shape[1]
    width = directions // dirs
    chunks = width // LANES
    far = far_ref.shape[1]

    def slice_of(step):
        return lax.rem(me + 1 + step, dirs)

    def interp_copies(j):
        for part in range(2):
            yield pltpu.make_async_copy(
                interp.at[:, pl.ds(pl.multiple_of(part * directions + j * width, LANES), width)],
                interp_vm.at[j, :, pl.ds(part * width, width)],
                interp_sem.at[part, j],
            )

    def near_copy(n):
        return pltpu.make_async_copy(near_matrix.at[n], near_vm.at[n], near_sem.at[n])

    agg_copy = pltpu.make_async_copy(aggregate, agg_vm, misc_sem.at[0])
    receive_copy = pltpu.make_async_copy(receive, receive_vm, misc_sem.at[1])
    trans_copy = pltpu.make_async_copy(translation, trans_vm, misc_sem.at[2])
    own_copy = pltpu.make_async_copy(currents, padded.at[pl.ds(reach, leaf_dev)], misc_sem.at[3])
    agg_copy.start()
    own_copy.start()

    @pl.loop(0, dirs)
    def _(step):
        for copy in interp_copies(slice_of(step)):
            copy.start()

    trans_copy.start()

    @pl.loop(0, slots)
    def _(n):
        near_copy(n).start()

    receive_copy.start()

    below = lax.rem(box + boxes - 1, boxes)
    above = lax.rem(box + 1, boxes)
    other = jnp.where(me < half, below, above)
    barrier = pltpu.get_barrier_semaphore()

    @pl.loop(1, dirs)
    def _(k):
        pl.semaphore_signal(
            barrier, inc=1, device_id=(box, lax.rem(me + k, dirs)), device_id_type=MESH
        )

    @pl.loop(0, half)
    def _(k):
        pl.semaphore_signal(barrier, inc=1, device_id=(below, half + k), device_id_type=MESH)
        pl.semaphore_signal(barrier, inc=1, device_id=(above, k), device_id_type=MESH)

    cosine[...] = jnp.cos(shift_angle[...])
    sine_part[...] = jnp.sin(shift_angle[...])
    first_leaf = (box * dirs + me) * leaf_dev - reach
    near_index[...] = (near_list[...] - first_leaf).astype(F32)

    pl.semaphore_wait(barrier, 2 * dirs - 1)

    left = (jnp.where(me == 0, below, box), lax.rem(me + dirs - 1, dirs))
    right = (jnp.where(me == dirs - 1, above, box), lax.rem(me + 1, dirs))
    to_left = pltpu.make_async_remote_copy(
        src_ref=currents.at[pl.ds(0, reach)],
        dst_ref=padded.at[pl.ds(reach + leaf_dev, reach)],
        send_sem=halo_send.at[0],
        recv_sem=halo_recv.at[0],
        device_id=left,
        device_id_type=MESH,
    )
    to_right = pltpu.make_async_remote_copy(
        src_ref=currents.at[pl.ds(leaf_dev - reach, reach)],
        dst_ref=padded.at[pl.ds(0, reach)],
        send_sem=halo_send.at[1],
        recv_sem=halo_recv.at[1],
        device_id=right,
        device_id_type=MESH,
    )
    to_left.start()
    to_right.start()

    agg_copy.wait()
    pattern[...] = jnp.dot(currents[...], agg_vm[...], preferred_element_type=F32).astype(BF16)

    my_slot = half + me
    other_slot = jnp.where(me < half, my_slot + dirs, my_slot - dirs)

    def up_copy(group, j, kind):
        return pltpu.make_async_remote_copy(
            src_ref=send_up.at[j],
            dst_ref=upper.at[(my_slot, other_slot)[kind]],
            send_sem=up_send.at[kind, j],
            recv_sem=up_recv.at[(my_slot, other_slot)[kind]],
            device_id=(group, j),
            device_id_type=MESH,
        )

    def forward(j):
        for copy in interp_copies(j):
            copy.wait()
        children = jnp.dot(pattern[...], interp_vm[j], preferred_element_type=F32)
        lanes = pl.ds(pl.multiple_of(j * width, LANES), width)
        cos, sin = cosine[:, lanes][None], sine_part[:, lanes][None]
        real = children[:, :width].reshape(own, 8, width)
        imag = children[:, width:].reshape(own, 8, width)
        real_part = jnp.sum(real * cos - imag * sin, axis=1)
        imag_part = jnp.sum(real * sin + imag * cos, axis=1)
        pieces = [
            part[:, t * LANES : (t + 1) * LANES]
            for part in (real_part, imag_part)
            for t in range(chunks)
        ]
        return jnp.concatenate(pieces, axis=0).astype(BF16)

    @pl.loop(0, dirs - 1)
    def _(step):
        j = slice_of(step)
        send_up[j] = forward(j)
        up_copy(other, j, 1).start()
        up_copy(box, j, 0).start()

    last = forward(me)
    send_up[me] = last
    up_copy(other, me, 1).start()
    upper[my_slot] = last

    trans_copy.wait()
    for s in range(4 * chunks):
        part, t = s // (2 * chunks), s % chunks
        operator[:, s, :] = trans_vm[:, part, t * LANES : (t + 1) * LANES]

    own_copy.wait()
    to_left.wait_recv()
    to_right.wait_recv()
    near_acc[...] = jnp.zeros_like(near_acc)

    def near_step(n):
        column_of = lax.broadcasted_iota(jnp.int32, near_index.shape, 1)
        column = jnp.sum(
            jnp.where(column_of == n, near_index[...], 0.0), axis=1, keepdims=True
        )
        row_of = lax.broadcasted_iota(jnp.int32, (leaf_dev, 2 * leaf_dev), 1).astype(F32)
        pick = jnp.where(row_of == column, 1.0, 0.0).astype(BF16)
        rows = jnp.dot(pick, padded[...], preferred_element_type=F32).astype(BF16)
        near_copy(n).wait()
        near_acc[...] += jnp.dot(rows, near_vm[n], preferred_element_type=F32)

    early = max(slots - dirs, 0)

    @pl.loop(0, early)
    def _(n):
        near_step(n)

    @pl.loop(1, 2 * dirs)
    def _(k):
        e = lax.rem(my_slot + k, 2 * dirs)
        pltpu.make_async_remote_copy(
            src_ref=upper.at[e],
            dst_ref=upper.at[e],
            send_sem=up_send.at[0, 0],
            recv_sem=up_recv.at[e],
            device_id=(box, me),
            device_id_type=MESH,
        ).wait_recv()

    @pl.loop(0, 2 * dirs)
    def _(e):
        block = upper[e].astype(F32)
        part = [block[own * c : own * (c + 1)] for c in range(2 * chunks)]
        rows = pl.ds(pl.multiple_of(e * own, own), own)
        turned = part + [-x for x in part[chunks:]] + part[:chunks]
        for s in range(4 * chunks):
            source[rows, s, :] = turned[s]

    def back_copy(j):
        return pltpu.make_async_remote_copy(
            src_ref=send_back.at[j],
            dst_ref=returned.at[me],
            send_sem=back_send.at[j],
            recv_sem=back_recv.at[me],
            device_id=(box, j),
            device_id_type=MESH,
        )

    def translate(j):
        @pl.loop(0, own)
        def _(r):
            p = j * own + r
            sums = [None] * 4
            for k in range(far):
                term = operator[kind_ref[p, k]] * source[far_ref[p, k]]
                sums[k % 4] = term if sums[k % 4] is None else sums[k % 4] + term
            total = (sums[0] + sums[1]) + (sums[2] + sums[3])
            local[p] = total[: 2 * chunks] + total[2 * chunks :]

        rows = pl.ds(pl.multiple_of(j * own, own), own)
        return jnp.concatenate([local[rows, c, :] for c in range(2 * chunks)], axis=0).astype(BF16)

    @pl.loop(0, dirs - 1)
    def _(step):
        j = slice_of(step)
        send_back[j] = translate(j)
        back_copy(j).start()

        @pl.when(early + step < slots)
        def _():
            near_step(early + step)

    returned[me] = translate(me)

    @pl.loop(early + dirs - 1, slots)
    def _(n):
        near_step(n)

    back_acc[...] = jnp.zeros_like(back_acc)

    def backward(j):
        block = returned[j].astype(F32)
        part = [block[own * c : own * (c + 1)] for c in range(2 * chunks)]
        real = jnp.concatenate(part[:chunks], axis=1)[:, None]
        imag = jnp.concatenate(part[chunks:], axis=1)[:, None]
        lanes = pl.ds(pl.multiple_of(j * width, LANES), width)
        cos, sin = cosine[:, lanes][None], sine_part[:, lanes][None]
        rot_real = (real * cos + imag * sin).reshape(leaf_dev, width)
        rot_imag = (imag * cos - real * sin).reshape(leaf_dev, width)
        received = jnp.concatenate([rot_real, rot_imag], axis=1).astype(BF16)
        back_acc[...] += lax.dot_general(
            received, interp_vm[j], (((1,), (1,)), ((), ())), preferred_element_type=F32
        )

    backward(me)

    @pl.loop(1, dirs)
    def _(k):
        j = lax.rem(me + dirs - k, dirs)
        pltpu.make_async_remote_copy(
            src_ref=returned.at[j],
            dst_ref=returned.at[j],
            send_sem=back_send.at[0],
            recv_sem=back_recv.at[j],
            device_id=(box, me),
            device_id_type=MESH,
        ).wait_recv()
        backward(j)

    receive_copy.wait()
    fields = jnp.dot(back_acc[...].astype(BF16), receive_vm[...], preferred_element_type=F32)
    out[...] = fields + near_acc[...]

    to_left.wait_send()
    to_right.wait_send()
    up_copy(other, me, 1).wait_send()

    @pl.loop(1, dirs)
    def _(k):
        j = lax.rem(me + k, dirs)
        up_copy(other, j, 1).wait_send()
        up_copy(box, j, 0).wait_send()
        back_copy(j).wait_send()


def on_device(
    boxes,
    dirs,
    currents,
    near_list,
    far_list,
    far_kind,
    aggregate,
    interp,
    receive,
    shift_angle,
    translation,
    near_matrix,
):
    leaf_dev, cur = currents.shape
    patterns = aggregate.shape[1]
    own = leaf_dev // 8
    upper_rows = own * dirs
    directions = shift_angle.shape[1]
    width = directions // dirs
    chunks = width // LANES
    kinds = translation.shape[0]
    slots = near_matrix.shape[0]
    first_row = lax.axis_index("box") * upper_rows
    my_far = lax.dynamic_slice_in_dim(far_list, first_row, upper_rows, 0)
    my_far = my_far - (first_row - upper_rows // 2)
    my_kind = lax.dynamic_slice_in_dim(far_kind, first_row, upper_rows, 0)
    smem = pl.BlockSpec(memory_space=pltpu.SMEM)
    vmem = pl.BlockSpec(memory_space=pltpu.VMEM)
    anywhere = pl.BlockSpec(memory_space=pl.ANY)
    message = (2 * chunks * own, LANES)
    dma = pltpu.SemaphoreType.DMA
    return pl.pallas_call(
        functools.partial(kernel, boxes, dirs),
        out_shape=jax.ShapeDtypeStruct((leaf_dev, receive.shape[1]), F32),
        in_specs=[smem, smem, vmem, vmem, vmem] + [anywhere] * 5,
        out_specs=vmem,
        scratch_shapes=[
            pltpu.VMEM(aggregate.shape, BF16),
            pltpu.VMEM((dirs, patterns, 2 * width), BF16),
            pltpu.VMEM(receive.shape, BF16),
            pltpu.VMEM(translation.shape, F32),
            pltpu.VMEM(near_matrix.shape, BF16),
            pltpu.VMEM((2 * leaf_dev, cur), BF16),
            pltpu.VMEM(near_list.shape, F32),
            pltpu.VMEM(shift_angle.shape, F32),
            pltpu.VMEM(shift_angle.shape, F32),
            pltpu.VMEM((leaf_dev, patterns), BF16),
            pltpu.VMEM((dirs,) + message, BF16),
            pltpu.VMEM((2 * dirs,) + message, BF16),
            pltpu.VMEM((kinds, 4 * chunks, LANES), F32),
            pltpu.VMEM((2 * upper_rows, 4 * chunks, LANES), F32),
            pltpu.VMEM((upper_rows, 2 * chunks, LANES), F32),
            pltpu.VMEM((dirs,) + message, BF16),
            pltpu.VMEM((dirs,) + message, BF16),
            pltpu.VMEM((leaf_dev, cur), F32),
            pltpu.VMEM((leaf_dev, patterns), F32),
            dma((4,)),
            dma((2, dirs)),
            dma((slots,)),
            dma((2,)),
            dma((2,)),
            dma((2, dirs)),
            dma((2 * dirs,)),
            dma((dirs,)),
            dma((dirs,)),
        ],
        compiler_params=pltpu.CompilerParams(
            collective_id=0, has_side_effects=True, vmem_limit_bytes=60 * 1024 * 1024
        ),
    )(
        my_far,
        my_kind,
        currents,
        near_list,
        shift_angle,
        aggregate,
        interp,
        receive,
        translation,
        near_matrix,
    )


def solution(mesh):
    placed = (
        P(("box", "dir"), None),
        P(("box", "dir"), None),
        P(),
        P(),
        P(),
        P(),
        P(),
        P(),
        P(None, None, "dir"),
        P(),
    )
    return jax.shard_map(
        functools.partial(on_device, mesh.shape["box"], mesh.shape["dir"]),
        mesh=mesh,
        in_specs=placed,
        out_specs=P(("box", "dir"), None),
        check_vma=False,
    )
```

```python
import functools

import jax
import jax.numpy as jnp
from jax import lax
from jax.experimental import pallas as pl
from jax.experimental.pallas import tpu as pltpu
from jax.sharding import PartitionSpec as P

MESH = pl.DeviceIdType.MESH
LANES = 128
F32 = jnp.float32
BF16 = jnp.bfloat16


def kernel(
    boxes,
    dirs,
    far_list,
    far_kind,
    currents,
    near_list,
    shift_angle,
    aggregate,
    interp,
    receive,
    translation,
    near_matrix,
    out,
    agg_vm,
    interp_vm,
    receive_vm,
    trans_vm,
    near_vm,
    far_ref,
    kind_ref,
    padded,
    near_rows,
    cosine,
    sine_part,
    pattern,
    send_up,
    upper,
    operator,
    source,
    local,
    send_back,
    returned,
    near_acc,
    back_acc,
    misc_sem,
    interp_sem,
    near_sem,
    halo_send,
    halo_recv,
    up_send,
    up_recv,
    back_send,
    back_recv,
):
    box = lax.axis_index("box")
    me = lax.axis_index("dir")
    leaf_dev, cur = currents.shape
    own = leaf_dev // 8
    reach = leaf_dev // 2
    half = dirs // 2
    slots = near_list.shape[0]
    groups, depth = near_vm.shape[:2]
    batch = slots // groups
    directions = shift_angle.shape[1]
    width = directions // dirs
    chunks = width // LANES
    far = far_ref.shape[0]

    def slice_of(step):
        return lax.rem(me + 1 + step, dirs)

    def interp_copies(j):
        for part in range(2):
            yield pltpu.make_async_copy(
                interp.at[:, pl.ds(pl.multiple_of(part * directions + j * width, LANES), width)],
                interp_vm.at[j, :, pl.ds(part * width, width)],
                interp_sem.at[part, j],
            )

    def near_copy(g):
        rows = pl.ds(pl.multiple_of(g * depth, depth), depth)
        return pltpu.make_async_copy(near_matrix.at[rows], near_vm.at[g], near_sem.at[g])

    agg_copy = pltpu.make_async_copy(aggregate, agg_vm, misc_sem.at[0])
    receive_copy = pltpu.make_async_copy(receive, receive_vm, misc_sem.at[1])
    trans_copy = pltpu.make_async_copy(translation, trans_vm, misc_sem.at[2])
    own_copy = pltpu.make_async_copy(currents, padded.at[pl.ds(reach, leaf_dev)], misc_sem.at[3])
    far_copy = pltpu.make_async_copy(far_list, far_ref, misc_sem.at[4])
    kind_copy = pltpu.make_async_copy(far_kind, kind_ref, misc_sem.at[5])
    agg_copy.start()
    own_copy.start()
    trans_copy.start()

    @pl.loop(0, dirs)
    def _(step):
        for copy in interp_copies(slice_of(step)):
            copy.start()

    far_copy.start()
    kind_copy.start()

    @pl.loop(0, groups)
    def _(g):
        near_copy(g).start()

    receive_copy.start()

    below = lax.rem(box + boxes - 1, boxes)
    above = lax.rem(box + 1, boxes)
    other = jnp.where(me < half, below, above)
    barrier = pltpu.get_barrier_semaphore()

    @pl.loop(1, dirs)
    def _(k):
        pl.semaphore_signal(
            barrier, inc=1, device_id=(box, lax.rem(me + k, dirs)), device_id_type=MESH
        )

    @pl.loop(0, half)
    def _(k):
        pl.semaphore_signal(barrier, inc=1, device_id=(below, half + k), device_id_type=MESH)
        pl.semaphore_signal(barrier, inc=1, device_id=(above, k), device_id_type=MESH)

    cosine[...] = jnp.cos(shift_angle[...])
    sine_part[...] = jnp.sin(shift_angle[...])

    agg_copy.wait()
    pattern[...] = jnp.dot(currents[...], agg_vm[...], preferred_element_type=F32).astype(BF16)

    pl.semaphore_wait(barrier, 2 * dirs - 1)

    left = (jnp.where(me == 0, below, box), lax.rem(me + dirs - 1, dirs))
    right = (jnp.where(me == dirs - 1, above, box), lax.rem(me + 1, dirs))
    to_left = pltpu.make_async_remote_copy(
        src_ref=currents.at[pl.ds(0, reach)],
        dst_ref=padded.at[pl.ds(reach + leaf_dev, reach)],
        send_sem=halo_send.at[0],
        recv_sem=halo_recv.at[0],
        device_id=left,
        device_id_type=MESH,
    )
    to_right = pltpu.make_async_remote_copy(
        src_ref=currents.at[pl.ds(leaf_dev - reach, reach)],
        dst_ref=padded.at[pl.ds(0, reach)],
        send_sem=halo_send.at[1],
        recv_sem=halo_recv.at[1],
        device_id=right,
        device_id_type=MESH,
    )
    to_left.start()
    to_right.start()

    trans_copy.wait()
    for s in range(4 * chunks):
        part, t = s // (2 * chunks), s % chunks
        operator[:, s, :] = trans_vm[:, part, t * LANES : (t + 1) * LANES]

    my_slot = half + me
    other_slot = jnp.where(me < half, my_slot + dirs, my_slot - dirs)

    def up_copy(group, j, kind):
        return pltpu.make_async_remote_copy(
            src_ref=send_up.at[j],
            dst_ref=upper.at[(my_slot, other_slot)[kind]],
            send_sem=up_send.at[kind, j],
            recv_sem=up_recv.at[(my_slot, other_slot)[kind]],
            device_id=(group, j),
            device_id_type=MESH,
        )

    def forward(j):
        children = jnp.dot(pattern[...], interp_vm[j], preferred_element_type=F32)
        lanes = pl.ds(pl.multiple_of(j * width, LANES), width)
        cos, sin = cosine[:, lanes][None], sine_part[:, lanes][None]
        real = children[:, :width].reshape(own, 8, width)
        imag = children[:, width:].reshape(own, 8, width)
        real_part = jnp.sum(real * cos - imag * sin, axis=1)
        imag_part = jnp.sum(real * sin + imag * cos, axis=1)
        pieces = [
            part[:, t * LANES : (t + 1) * LANES]
            for part in (real_part, imag_part)
            for t in range(chunks)
        ]
        return jnp.concatenate(pieces, axis=0).astype(BF16)

    def forward_pair(first, second):
        for j in (first, second):
            for copy in interp_copies(j):
                copy.wait()
        one, two = forward(first), forward(second)
        send_up[first] = one
        send_up[second] = two
        up_copy(other, first, 1).start()
        up_copy(box, first, 0).start()
        up_copy(other, second, 1).start()
        return two

    @pl.loop(0, dirs // 2 - 1)
    def _(step):
        second = slice_of(2 * step + 1)
        forward_pair(slice_of(2 * step), second)
        up_copy(box, second, 0).start()

    upper[my_slot] = forward_pair(slice_of(dirs - 2), me)

    own_copy.wait()
    to_left.wait_recv()
    to_right.wait_recv()
    first_leaf = (box * dirs + me) * leaf_dev - reach
    index = (near_list[...] - first_leaf).astype(F32).T
    row_of = lax.broadcasted_iota(jnp.int32, (leaf_dev, 2 * leaf_dev), 1).astype(F32)
    for n in range(slots):
        pick = jnp.where(row_of == index[:, n : n + 1], 1.0, 0.0).astype(BF16)
        rows = jnp.dot(pick, padded[...], preferred_element_type=F32).astype(BF16)
        near_rows[n // batch, :, (n % batch) * cur : (n % batch + 1) * cur] = rows

    near_acc[...] = jnp.zeros_like(near_acc)

    def near_group(g):
        near_copy(g).wait()
        near_acc[...] += jnp.dot(near_rows[g], near_vm[g], preferred_element_type=F32)

    early = (groups + 1) // 2

    @pl.loop(0, early)
    def _(g):
        near_group(g)

    far_copy.wait()
    kind_copy.wait()

    @pl.loop(1, 2 * dirs)
    def _(k):
        e = lax.rem(my_slot + k, 2 * dirs)
        pltpu.make_async_remote_copy(
            src_ref=upper.at[e],
            dst_ref=upper.at[e],
            send_sem=up_send.at[0, 0],
            recv_sem=up_recv.at[e],
            device_id=(box, me),
            device_id_type=MESH,
        ).wait_recv()

    def spread(e):
        block = upper[e].astype(F32)
        part = [block[own * c : own * (c + 1)] for c in range(2 * chunks)]
        place = lax.rem(e + box * dirs + 2 * dirs - half, 2 * dirs)
        rows = pl.ds(pl.multiple_of(place * own, own), own)
        turned = part + [-x for x in part[chunks:]] + part[:chunks]
        for s in range(4 * chunks):
            source[rows, s, :] = turned[s]

    @pl.loop(0, dirs // 2)
    def _(quarter):
        for k in range(4):
            spread(4 * quarter + k)

    def back_copy(j):
        return pltpu.make_async_remote_copy(
            src_ref=send_back.at[j],
            dst_ref=returned.at[me],
            send_sem=back_send.at[j],
            recv_sem=back_recv.at[me],
            device_id=(box, j),
            device_id_type=MESH,
        )

    first_row = box * dirs * own
    window = 2 * dirs * own

    def in_window(row):
        return row & (window - 1) if window & (window - 1) == 0 else lax.rem(row, window)

    def translate(j):
        for r in range(own):
            p = j * own + r
            sums = [None] * 2
            for k in range(far):
                kind = kind_ref[k, first_row + p]
                row = in_window(far_ref[k, first_row + p])
                term = operator[kind] * source[row]
                sums[k % 2] = term if sums[k % 2] is None else sums[k % 2] + term
            total = sums[0] + sums[1]
            local[p] = total[: 2 * chunks] + total[2 * chunks :]

        rows = pl.ds(pl.multiple_of(j * own, own), own)
        return jnp.concatenate([local[rows, c, :] for c in range(2 * chunks)], axis=0).astype(BF16)

    @pl.loop(0, dirs - 1)
    def _(step):
        j = slice_of(step)
        send_back[j] = translate(j)
        back_copy(j).start()

    returned[me] = translate(me)

    @pl.loop(early, groups)
    def _(g):
        near_group(g)

    back_acc[...] = jnp.zeros_like(back_acc)

    def received(j):
        block = returned[j].astype(F32)
        part = [block[own * c : own * (c + 1)] for c in range(2 * chunks)]
        real = jnp.concatenate(part[:chunks], axis=1)[:, None]
        imag = jnp.concatenate(part[chunks:], axis=1)[:, None]
        lanes = pl.ds(pl.multiple_of(j * width, LANES), width)
        cos, sin = cosine[:, lanes][None], sine_part[:, lanes][None]
        rot_real = (real * cos + imag * sin).reshape(leaf_dev, width)
        rot_imag = (imag * cos - real * sin).reshape(leaf_dev, width)
        return jnp.concatenate([rot_real, rot_imag], axis=1).astype(BF16)

    def back_wait(j):
        pltpu.make_async_remote_copy(
            src_ref=returned.at[j],
            dst_ref=returned.at[j],
            send_sem=back_send.at[0],
            recv_sem=back_recv.at[j],
            device_id=(box, me),
            device_id_type=MESH,
        ).wait_recv()

    def back_pair(first, second):
        total = None
        for j in (first, second):
            term = lax.dot_general(
                received(j), interp_vm[j], (((1,), (1,)), ((), ())), preferred_element_type=F32
            )
            total = term if total is None else total + term
        back_acc[...] += total

    nearest = lax.rem(me + dirs - 1, dirs)
    back_wait(nearest)
    back_pair(me, nearest)

    @pl.loop(1, dirs // 2)
    def _(k):
        first = lax.rem(me + dirs - 2 * k, dirs)
        second = lax.rem(me + dirs - 2 * k - 1, dirs)
        back_wait(first)
        back_wait(second)
        back_pair(first, second)

    receive_copy.wait()
    fields = jnp.dot(back_acc[...].astype(BF16), receive_vm[...], preferred_element_type=F32)
    out[...] = fields + near_acc[...]

    to_left.wait_send()
    to_right.wait_send()
    up_copy(other, me, 1).wait_send()

    @pl.loop(1, dirs)
    def _(k):
        j = lax.rem(me + k, dirs)
        up_copy(other, j, 1).wait_send()
        up_copy(box, j, 0).wait_send()
        back_copy(j).wait_send()


def on_device(
    boxes,
    dirs,
    currents,
    near_list,
    far_list,
    far_kind,
    aggregate,
    interp,
    receive,
    shift_angle,
    translation,
    near_matrix,
):
    leaf_dev, cur = currents.shape
    patterns = aggregate.shape[1]
    own = leaf_dev // 8
    upper_rows = own * dirs
    directions = shift_angle.shape[1]
    width = directions // dirs
    chunks = width // LANES
    kinds = translation.shape[0]
    slots = near_matrix.shape[0]
    batch = next(size for size in (3, 2, 1) if slots % size == 0)
    groups, depth = slots // batch, batch * cur
    vmem = pl.BlockSpec(memory_space=pltpu.VMEM)
    anywhere = pl.BlockSpec(memory_space=pltpu.HBM)
    message = (2 * chunks * own, LANES)
    dma = pltpu.SemaphoreType.DMA
    return pl.pallas_call(
        functools.partial(kernel, boxes, dirs),
        out_shape=jax.ShapeDtypeStruct((leaf_dev, receive.shape[1]), F32),
        in_specs=[anywhere] * 2 + [vmem] * 3 + [anywhere] * 5,
        out_specs=vmem,
        scratch_shapes=[
            pltpu.VMEM(aggregate.shape, BF16),
            pltpu.VMEM((dirs, patterns, 2 * width), BF16),
            pltpu.VMEM(receive.shape, BF16),
            pltpu.VMEM(translation.shape, F32),
            pltpu.VMEM((groups, depth, near_matrix.shape[2]), BF16),
            pltpu.SMEM(far_list.shape[::-1], jnp.int32),
            pltpu.SMEM(far_kind.shape[::-1], jnp.int32),
            pltpu.VMEM((2 * leaf_dev, cur), BF16),
            pltpu.VMEM((groups, leaf_dev, depth), BF16),
            pltpu.VMEM(shift_angle.shape, F32),
            pltpu.VMEM(shift_angle.shape, F32),
            pltpu.VMEM((leaf_dev, patterns), BF16),
            pltpu.VMEM((dirs,) + message, BF16),
            pltpu.VMEM((2 * dirs,) + message, BF16),
            pltpu.VMEM((kinds, 4 * chunks, LANES), F32),
            pltpu.VMEM((2 * upper_rows, 4 * chunks, LANES), F32),
            pltpu.VMEM((upper_rows, 2 * chunks, LANES), F32),
            pltpu.VMEM((dirs,) + message, BF16),
            pltpu.VMEM((dirs,) + message, BF16),
            pltpu.VMEM((leaf_dev, cur), F32),
            pltpu.VMEM((leaf_dev, patterns), F32),
            dma((6,)),
            dma((2, dirs)),
            dma((groups,)),
            dma((2,)),
            dma((2,)),
            dma((2, dirs)),
            dma((2 * dirs,)),
            dma((dirs,)),
            dma((dirs,)),
        ],
        compiler_params=pltpu.CompilerParams(
            collective_id=0, has_side_effects=True, vmem_limit_bytes=60 * 1024 * 1024
        ),
    )(
        far_list.T,
        far_kind.T,
        currents,
        near_list.T,
        shift_angle,
        aggregate,
        interp,
        receive,
        translation,
        near_matrix.reshape(-1, near_matrix.shape[2]),
    )


def solution(mesh):
    placed = (
        P(("box", "dir"), None),
        P(("box", "dir"), None),
        P(),
        P(),
        P(),
        P(),
        P(),
        P(),
        P(None, None, "dir"),
        P(),
    )
    return jax.shard_map(
        functools.partial(on_device, mesh.shape["box"], mesh.shape["dir"]),
        mesh=mesh,
        in_specs=placed,
        out_specs=P(("box", "dir"), None),
        check_vma=False,
    )
```

```python
import functools

import jax
import jax.numpy as jnp
from jax import lax
from jax.experimental import pallas as pl
from jax.experimental.pallas import tpu as pltpu
from jax.sharding import PartitionSpec as P

MESH = pl.DeviceIdType.MESH
LANES = 128
F32 = jnp.float32
BF16 = jnp.bfloat16


def kernel(
    boxes,
    dirs,
    far_list,
    far_kind,
    currents,
    near_list,
    shift_angle,
    aggregate,
    interp,
    receive,
    translation,
    near_matrix,
    out,
    agg_vm,
    interp_vm,
    receive_vm,
    trans_vm,
    near_vm,
    far_ref,
    kind_ref,
    padded,
    near_rows,
    cosine,
    sine_part,
    pattern,
    send_up,
    upper,
    operator,
    source,
    local,
    send_back,
    returned,
    near_acc,
    back_acc,
    misc_sem,
    interp_sem,
    near_sem,
    halo_send,
    halo_recv,
    up_send,
    up_recv,
    back_send,
    back_recv,
):
    box = lax.axis_index("box")
    me = lax.axis_index("dir")
    leaf_dev, cur = currents.shape
    own = leaf_dev // 8
    reach = leaf_dev // 2
    half = dirs // 2
    slots = near_list.shape[0]
    groups, depth = near_vm.shape[:2]
    batch = slots // groups
    directions = shift_angle.shape[1]
    width = directions // dirs
    chunks = width // LANES
    far = far_ref.shape[0]

    def slice_of(step):
        return lax.rem(me + 1 + step, dirs)

    def interp_copies(j):
        for part in range(2):
            yield pltpu.make_async_copy(
                interp.at[:, pl.ds(pl.multiple_of(part * directions + j * width, LANES), width)],
                interp_vm.at[j, :, pl.ds(part * width, width)],
                interp_sem.at[part, j],
            )

    def near_copy(g):
        rows = pl.ds(pl.multiple_of(g * depth, depth), depth)
        return pltpu.make_async_copy(near_matrix.at[rows], near_vm.at[g], near_sem.at[g])

    agg_copy = pltpu.make_async_copy(aggregate, agg_vm, misc_sem.at[0])
    receive_copy = pltpu.make_async_copy(receive, receive_vm, misc_sem.at[1])
    trans_copy = pltpu.make_async_copy(translation, trans_vm, misc_sem.at[2])
    own_copy = pltpu.make_async_copy(currents, padded.at[pl.ds(reach, leaf_dev)], misc_sem.at[3])
    far_copy = pltpu.make_async_copy(far_list, far_ref, misc_sem.at[4])
    kind_copy = pltpu.make_async_copy(far_kind, kind_ref, misc_sem.at[5])
    agg_copy.start()
    own_copy.start()
    trans_copy.start()

    @pl.loop(0, dirs)
    def _(step):
        for copy in interp_copies(slice_of(step)):
            copy.start()

    far_copy.start()
    kind_copy.start()

    @pl.loop(0, groups)
    def _(g):
        near_copy(g).start()

    receive_copy.start()

    below = lax.rem(box + boxes - 1, boxes)
    above = lax.rem(box + 1, boxes)
    other = jnp.where(me < half, below, above)
    barrier = pltpu.get_barrier_semaphore()

    @pl.loop(1, dirs)
    def _(k):
        pl.semaphore_signal(
            barrier, inc=1, device_id=(box, lax.rem(me + k, dirs)), device_id_type=MESH
        )

    @pl.loop(0, half)
    def _(k):
        pl.semaphore_signal(barrier, inc=1, device_id=(below, half + k), device_id_type=MESH)
        pl.semaphore_signal(barrier, inc=1, device_id=(above, k), device_id_type=MESH)

    cosine[...] = jnp.cos(shift_angle[...])
    sine_part[...] = jnp.sin(shift_angle[...])

    agg_copy.wait()
    pattern[...] = jnp.dot(currents[...], agg_vm[...], preferred_element_type=F32).astype(BF16)

    pl.semaphore_wait(barrier, 2 * dirs - 1)

    left = (jnp.where(me == 0, below, box), lax.rem(me + dirs - 1, dirs))
    right = (jnp.where(me == dirs - 1, above, box), lax.rem(me + 1, dirs))
    to_left = pltpu.make_async_remote_copy(
        src_ref=currents.at[pl.ds(0, reach)],
        dst_ref=padded.at[pl.ds(reach + leaf_dev, reach)],
        send_sem=halo_send.at[0],
        recv_sem=halo_recv.at[0],
        device_id=left,
        device_id_type=MESH,
    )
    to_right = pltpu.make_async_remote_copy(
        src_ref=currents.at[pl.ds(leaf_dev - reach, reach)],
        dst_ref=padded.at[pl.ds(0, reach)],
        send_sem=halo_send.at[1],
        recv_sem=halo_recv.at[1],
        device_id=right,
        device_id_type=MESH,
    )
    to_left.start()
    to_right.start()

    trans_copy.wait()
    for s in range(4 * chunks):
        part, t = s // (2 * chunks), s % chunks
        operator[:, s, :] = trans_vm[:, part, t * LANES : (t + 1) * LANES]

    my_slot = half + me
    other_slot = jnp.where(me < half, my_slot + dirs, my_slot - dirs)

    def up_copy(group, j, kind):
        return pltpu.make_async_remote_copy(
            src_ref=send_up.at[j],
            dst_ref=upper.at[(my_slot, other_slot)[kind]],
            send_sem=up_send.at[kind, j],
            recv_sem=up_recv.at[(my_slot, other_slot)[kind]],
            device_id=(group, j),
            device_id_type=MESH,
        )

    def forward(j):
        children = jnp.dot(pattern[...], interp_vm[j], preferred_element_type=F32)
        lanes = pl.ds(pl.multiple_of(j * width, LANES), width)
        cos, sin = cosine[:, lanes][None], sine_part[:, lanes][None]
        real = children[:, :width].reshape(own, 8, width)
        imag = children[:, width:].reshape(own, 8, width)
        real_part = jnp.sum(real * cos - imag * sin, axis=1)
        imag_part = jnp.sum(real * sin + imag * cos, axis=1)
        pieces = [
            part[:, t * LANES : (t + 1) * LANES]
            for part in (real_part, imag_part)
            for t in range(chunks)
        ]
        return jnp.concatenate(pieces, axis=0).astype(BF16)

    def forward_pair(first, second):
        for j in (first, second):
            for copy in interp_copies(j):
                copy.wait()
        one, two = forward(first), forward(second)
        send_up[first] = one
        send_up[second] = two
        up_copy(other, first, 1).start()
        up_copy(box, first, 0).start()
        up_copy(other, second, 1).start()
        return two

    @pl.loop(0, dirs // 2 - 1)
    def _(step):
        second = slice_of(2 * step + 1)
        forward_pair(slice_of(2 * step), second)
        up_copy(box, second, 0).start()

    upper[my_slot] = forward_pair(slice_of(dirs - 2), me)

    own_copy.wait()
    to_left.wait_recv()
    to_right.wait_recv()
    first_leaf = (box * dirs + me) * leaf_dev - reach
    index = (near_list[...] - first_leaf).astype(F32).T
    row_of = lax.broadcasted_iota(jnp.int32, (leaf_dev, 2 * leaf_dev), 1).astype(F32)
    for n in range(slots):
        pick = jnp.where(row_of == index[:, n : n + 1], 1.0, 0.0).astype(BF16)
        rows = jnp.dot(pick, padded[...], preferred_element_type=F32).astype(BF16)
        near_rows[n // batch, :, (n % batch) * cur : (n % batch + 1) * cur] = rows

    near_acc[...] = jnp.zeros_like(near_acc)

    def near_group(g):
        near_copy(g).wait()
        near_acc[...] += jnp.dot(near_rows[g], near_vm[g], preferred_element_type=F32)

    early = max(groups - 2, 1)

    @pl.loop(0, early)
    def _(g):
        near_group(g)

    far_copy.wait()
    kind_copy.wait()

    @pl.loop(1, 2 * dirs)
    def _(k):
        e = lax.rem(my_slot + k, 2 * dirs)
        pltpu.make_async_remote_copy(
            src_ref=upper.at[e],
            dst_ref=upper.at[e],
            send_sem=up_send.at[0, 0],
            recv_sem=up_recv.at[e],
            device_id=(box, me),
            device_id_type=MESH,
        ).wait_recv()

    def spread(e):
        block = upper[e].astype(F32)
        part = [block[own * c : own * (c + 1)] for c in range(2 * chunks)]
        place = lax.rem(e + box * dirs + 2 * dirs - half, 2 * dirs)
        rows = pl.ds(pl.multiple_of(place * own, own), own)
        turned = part + [-x for x in part[chunks:]] + part[:chunks]
        for s in range(4 * chunks):
            source[rows, s, :] = turned[s]

    @pl.loop(0, dirs // 2)
    def _(quarter):
        for k in range(4):
            spread(4 * quarter + k)

    def back_copy(j):
        return pltpu.make_async_remote_copy(
            src_ref=send_back.at[j],
            dst_ref=returned.at[me],
            send_sem=back_send.at[j],
            recv_sem=back_recv.at[me],
            device_id=(box, j),
            device_id_type=MESH,
        )

    first_row = box * dirs * own
    window = 2 * dirs * own

    def in_window(row):
        return row & (window - 1) if window & (window - 1) == 0 else lax.rem(row, window)

    def translate(j):
        for r in range(own):
            p = j * own + r
            sums = [None] * 2
            for k in range(far):
                kind = kind_ref[k, first_row + p]
                row = in_window(far_ref[k, first_row + p])
                term = operator[kind] * source[row]
                sums[k % 2] = term if sums[k % 2] is None else sums[k % 2] + term
            total = sums[0] + sums[1]
            local[p] = total[: 2 * chunks] + total[2 * chunks :]

        rows = pl.ds(pl.multiple_of(j * own, own), own)
        return jnp.concatenate([local[rows, c, :] for c in range(2 * chunks)], axis=0).astype(BF16)

    @pl.loop(0, dirs - 1)
    def _(step):
        j = slice_of(step)
        send_back[j] = translate(j)
        back_copy(j).start()

    returned[me] = translate(me)

    @pl.loop(early, groups)
    def _(g):
        near_group(g)

    back_acc[...] = jnp.zeros_like(back_acc)

    def received(j):
        block = returned[j].astype(F32)
        part = [block[own * c : own * (c + 1)] for c in range(2 * chunks)]
        real = jnp.concatenate(part[:chunks], axis=1)[:, None]
        imag = jnp.concatenate(part[chunks:], axis=1)[:, None]
        lanes = pl.ds(pl.multiple_of(j * width, LANES), width)
        cos, sin = cosine[:, lanes][None], sine_part[:, lanes][None]
        rot_real = (real * cos + imag * sin).reshape(leaf_dev, width)
        rot_imag = (imag * cos - real * sin).reshape(leaf_dev, width)
        return jnp.concatenate([rot_real, rot_imag], axis=1).astype(BF16)

    def back_wait(j):
        pltpu.make_async_remote_copy(
            src_ref=returned.at[j],
            dst_ref=returned.at[j],
            send_sem=back_send.at[0],
            recv_sem=back_recv.at[j],
            device_id=(box, me),
            device_id_type=MESH,
        ).wait_recv()

    def back_pair(first, second):
        total = None
        for j in (first, second):
            term = lax.dot_general(
                received(j), interp_vm[j], (((1,), (1,)), ((), ())), preferred_element_type=F32
            )
            total = term if total is None else total + term
        back_acc[...] += total

    nearest = lax.rem(me + dirs - 1, dirs)
    back_wait(nearest)
    back_pair(me, nearest)

    for k in range(1, dirs // 2):
        first = lax.rem(me + dirs - 2 * k, dirs)
        second = lax.rem(me + dirs - 2 * k - 1, dirs)
        back_wait(first)
        back_wait(second)
        back_pair(first, second)

    receive_copy.wait()
    fields = jnp.dot(back_acc[...].astype(BF16), receive_vm[...], preferred_element_type=F32)
    out[...] = fields + near_acc[...]

    to_left.wait_send()
    to_right.wait_send()
    up_copy(other, me, 1).wait_send()

    @pl.loop(1, dirs)
    def _(k):
        j = lax.rem(me + k, dirs)
        up_copy(other, j, 1).wait_send()
        up_copy(box, j, 0).wait_send()
        back_copy(j).wait_send()


def on_device(
    boxes,
    dirs,
    currents,
    near_list,
    far_list,
    far_kind,
    aggregate,
    interp,
    receive,
    shift_angle,
    translation,
    near_matrix,
):
    leaf_dev, cur = currents.shape
    patterns = aggregate.shape[1]
    own = leaf_dev // 8
    upper_rows = own * dirs
    directions = shift_angle.shape[1]
    width = directions // dirs
    chunks = width // LANES
    kinds = translation.shape[0]
    slots = near_matrix.shape[0]
    batch = next(size for size in (3, 2, 1) if slots % size == 0)
    groups, depth = slots // batch, batch * cur
    vmem = pl.BlockSpec(memory_space=pltpu.VMEM)
    anywhere = pl.BlockSpec(memory_space=pltpu.HBM)
    message = (2 * chunks * own, LANES)
    dma = pltpu.SemaphoreType.DMA
    return pl.pallas_call(
        functools.partial(kernel, boxes, dirs),
        out_shape=jax.ShapeDtypeStruct((leaf_dev, receive.shape[1]), F32),
        in_specs=[anywhere] * 2 + [vmem] * 3 + [anywhere] * 5,
        out_specs=vmem,
        scratch_shapes=[
            pltpu.VMEM(aggregate.shape, BF16),
            pltpu.VMEM((dirs, patterns, 2 * width), BF16),
            pltpu.VMEM(receive.shape, BF16),
            pltpu.VMEM(translation.shape, F32),
            pltpu.VMEM((groups, depth, near_matrix.shape[2]), BF16),
            pltpu.SMEM(far_list.shape[::-1], jnp.int32),
            pltpu.SMEM(far_kind.shape[::-1], jnp.int32),
            pltpu.VMEM((2 * leaf_dev, cur), BF16),
            pltpu.VMEM((groups, leaf_dev, depth), BF16),
            pltpu.VMEM(shift_angle.shape, F32),
            pltpu.VMEM(shift_angle.shape, F32),
            pltpu.VMEM((leaf_dev, patterns), BF16),
            pltpu.VMEM((dirs,) + message, BF16),
            pltpu.VMEM((2 * dirs,) + message, BF16),
            pltpu.VMEM((kinds, 4 * chunks, LANES), F32),
            pltpu.VMEM((2 * upper_rows, 4 * chunks, LANES), F32),
            pltpu.VMEM((upper_rows, 2 * chunks, LANES), F32),
            pltpu.VMEM((dirs,) + message, BF16),
            pltpu.VMEM((dirs,) + message, BF16),
            pltpu.VMEM((leaf_dev, cur), F32),
            pltpu.VMEM((leaf_dev, patterns), F32),
            dma((6,)),
            dma((2, dirs)),
            dma((groups,)),
            dma((2,)),
            dma((2,)),
            dma((2, dirs)),
            dma((2 * dirs,)),
            dma((dirs,)),
            dma((dirs,)),
        ],
        compiler_params=pltpu.CompilerParams(
            collective_id=0, has_side_effects=True, vmem_limit_bytes=60 * 1024 * 1024
        ),
    )(
        far_list.T,
        far_kind.T,
        currents,
        near_list.T,
        shift_angle,
        aggregate,
        interp,
        receive,
        translation,
        near_matrix.reshape(-1, near_matrix.shape[2]),
    )


def solution(mesh):
    placed = (
        P(("box", "dir"), None),
        P(("box", "dir"), None),
        P(),
        P(),
        P(),
        P(),
        P(),
        P(),
        P(None, None, "dir"),
        P(),
    )
    return jax.shard_map(
        functools.partial(on_device, mesh.shape["box"], mesh.shape["dir"]),
        mesh=mesh,
        in_specs=placed,
        out_specs=P(("box", "dir"), None),
        check_vma=False,
    )
```
